32 devices in a mesh: row: 16 (over z, y, x), col: 2 (over core).
Axes of the slice: x: 2, y: 2, z: 4, core: 2. Of those that a mesh axis runs over, the one named last changes fastest.
Arguments:
- top_tensor: bfloat16 [2304, 2304], P('row', 'col'), may hold values from -3 to 3
- bottom_tensor: bfloat16 [2304, 2304], P(('col', 'row')), may hold values from -3 to 3
- left_proj: bfloat16 [2304, 48], replicated, may hold values from -0.125 to 0.125
- right_proj: bfloat16 [2304, 48], replicated, may hold values from -0.125 to 0.125
Outputs:
- coarse: bfloat16 [2304, 2304], P(('col', 'row'))
The draws below stay inside these ranges and needn't reach their ends.
All inputs are finite; a program needn't handle non-finite values.
Results may differ from the reference program's by a relative error of at most 0.0065.
Values may be sent and summed in bfloat16 or wider, within the bound.
A program may use at most 128 MiB of HBM per device.

```python
import jax
import jax.numpy as jnp
from jax import lax

CHI = 48
N_COL = 2


def block_scale(stream_key, shape, pieces, smallest, largest):
    def one(dim, shards_of):
        heights = jax.random.uniform(jax.random.fold_in(jax.random.fold_in(stream_key, 6), dim), (shards_of,), jnp.float32, smallest / len(pieces), largest / len(pieces))
        return jnp.repeat(jnp.exp(heights), shape[dim] // shards_of).reshape((-1,) + (1,) * (len(shape) - dim - 1))

    level = one(*pieces[0])
    for cut in pieces[1:]:
        level = level * one(*cut)
    return level


def bell_draw(stream_key, shape, spread, limit, pieces=(), kind=jnp.bfloat16):
    result = jax.random.normal(stream_key, shape, jnp.float32) * spread
    if len(pieces) > 0:
        result = block_scale(stream_key, shape, pieces, -0.22, 0.18) * result
    return jnp.clip(result, min=-limit, max=limit).astype(kind)


def setup_inputs(seed: int = 0) -> dict:
    keys = jax.random.split(jax.random.key(seed), 5)
    return {
        "top_tensor": bell_draw(keys[0], (CHI * CHI, CHI * CHI), 0.38, 3.0, ((0, 16), (1, 2))),
        "bottom_tensor": bell_draw(keys[1], (CHI * CHI, CHI * CHI), 0.38, 3.0, ((0, 32),)),
        "left_proj": bell_draw(keys[2], (CHI * CHI, CHI), (CHI * CHI) ** -0.5, 0.125),
        "right_proj": bell_draw(keys[3], (CHI * CHI, CHI), (CHI * CHI) ** -0.5, 0.125),
    }


def reference(top_tensor, bottom_tensor, left_proj, right_proj):
    bond_dim = CHI
    block_len = CHI // N_COL
    left_table = left_proj.reshape(bond_dim, bond_dim, bond_dim).astype(jnp.float32)
    upper_part = top_tensor.reshape(bond_dim, bond_dim, bond_dim, bond_dim)

    def one_up(upper_slice):
        weighted = jnp.einsum("rml,lka->ramk", upper_slice.astype(jnp.float32), left_table, precision=lax.Precision.HIGHEST)
        weighted = weighted.astype(jnp.bfloat16).reshape(bond_dim * bond_dim, bond_dim * bond_dim)
        running = jnp.zeros((bond_dim * bond_dim, bond_dim), jnp.float32)
        for block_idx in range(N_COL):
            first = block_idx * block_len * bond_dim
            last = first + block_len * bond_dim
            paired = jnp.dot(weighted[:, first:last], bottom_tensor[first:last], preferred_element_type=jnp.float32)
            paired = paired.astype(jnp.bfloat16).reshape(bond_dim, bond_dim, bond_dim, bond_dim)
            paired = paired.transpose(1, 2, 0, 3).reshape(bond_dim * bond_dim, bond_dim * bond_dim)
            running = running + jnp.dot(paired, right_proj, preferred_element_type=jnp.float32)
        return running.reshape(bond_dim, bond_dim, bond_dim)

    per_up = lax.map(one_up, upper_part)
    coarse = per_up.transpose(2, 1, 0, 3).reshape(bond_dim * bond_dim, bond_dim * bond_dim)
    return coarse.astype(jnp.bfloat16)
```

```python
import jax
import jax.numpy as jnp
from jax import lax
from jax.experimental import pallas as pl
from jax.experimental.pallas import tpu as pltpu
from jax.sharding import PartitionSpec as P


def place_rows(arrived, window, rows_here, bond_dim, row_count):
    slot_ids = jnp.arange(row_count * window, dtype=jnp.int32)
    source_dev = slot_ids // window
    target_upper = source_dev * rows_here // bond_dim + slot_ids % window
    placing = (target_upper[:, None] == jnp.arange(bond_dim, dtype=jnp.int32)[None, :]).astype(
        jnp.float32
    )
    return jnp.einsum("rsb,su->rub", arrived, placing, precision=lax.Precision.HIGHEST)


def local_windowed(top_tensor, bottom_tensor, left_proj, right_proj):
    bond_dim = right_proj.shape[1]
    rows_here = top_tensor.shape[0]
    block_len = top_tensor.shape[1] // bond_dim
    lower_rows = lax.all_gather(bottom_tensor, "row", axis=0, tiled=True)
    left_table = left_proj.reshape(bond_dim, bond_dim, bond_dim)
    upper_part = top_tensor.reshape(rows_here, block_len, bond_dim)
    weighted = jnp.einsum(
        "rml,lka->ramk", upper_part, left_table, preferred_element_type=jnp.float32
    )
    weighted = weighted.astype(jnp.bfloat16).reshape(rows_here * bond_dim, block_len * bond_dim)
    window = rows_here // bond_dim + 2
    row_count = lax.axis_size("row")
    start_row = lax.axis_index("row") * rows_here
    first_upper = start_row // bond_dim
    offset_rows = start_row - first_upper * bond_dim
    group_size = 8
    groups = bond_dim // group_size
    column_sets = lower_rows.reshape(block_len * bond_dim, groups, group_size * bond_dim).transpose(
        1, 0, 2
    )

    def one_group(columns):
        product_part = jnp.dot(weighted, columns, preferred_element_type=jnp.float32).astype(
            jnp.bfloat16
        )
        product_part = product_part.reshape(rows_here, bond_dim, group_size, bond_dim)
        padded = jnp.zeros((window * bond_dim, bond_dim, group_size, bond_dim), jnp.bfloat16)
        padded = lax.dynamic_update_slice_in_dim(padded, product_part, offset_rows, 0)
        regrid = padded.reshape(window, bond_dim, bond_dim, group_size, bond_dim).transpose(
            0, 2, 3, 1, 4
        )
        regrid = regrid.reshape(window * bond_dim * group_size, bond_dim * bond_dim)
        projected = jnp.dot(regrid, right_proj, preferred_element_type=jnp.float32)
        return projected.reshape(window, bond_dim, group_size, bond_dim)

    stacked = lax.map(one_group, column_sets)
    per_down = stacked.transpose(0, 3, 2, 1, 4).reshape(bond_dim, bond_dim, window, bond_dim)
    summed = lax.psum_scatter(per_down, "col", scatter_dimension=0, tiled=True)
    summed = summed.reshape(summed.shape[0] * bond_dim, window, bond_dim)
    arrived = lax.all_to_all(summed, "row", split_axis=0, concat_axis=1, tiled=True)
    combined = place_rows(arrived, window, rows_here, bond_dim, row_count)
    out_rows = combined.shape[0]
    return combined.reshape(out_rows, bond_dim * bond_dim).astype(jnp.bfloat16)


TILE = 256
CHUNKS = 2
VMEM_LIMIT = 60 * 1024 * 1024


def tiled_blocks(proj, group):
    lanes = group * proj.shape[2]
    pad = jnp.zeros(proj.shape[:2] + (TILE - lanes,), proj.dtype)
    return jnp.concatenate([proj] * group + [pad], axis=2)


def block_diagonal(tiled, group):
    size = tiled.shape[0]
    lane_block = lax.broadcasted_iota(jnp.int32, tiled.shape, 1) // size
    zero = jnp.zeros_like(tiled)
    rows = [jnp.where(lane_block == k, tiled, zero) for k in range(group)]
    rows.append(jnp.zeros((TILE - group * size, TILE), tiled.dtype))
    return jnp.concatenate(rows, axis=0)


def weight_upper(upper_part, left_tiled, bond_dim, ups, group):
    rows, padded = upper_part.shape
    tiles = padded // TILE
    out_rows = ups * bond_dim
    halves = TILE // 128

    def body(upper_ref, left_ref, out_ref, scratch):
        def one_left(a, carry):
            weights = block_diagonal(left_ref[a], group)
            part = jnp.dot(upper_ref[...], weights, preferred_element_type=jnp.float32)
            for up in range(ups):
                for h in range(halves):
                    scratch.at[h][pl.ds(up * bond_dim + a, bond_dim, stride=out_rows), :] = part[
                        up * bond_dim : (up + 1) * bond_dim, h * 128 : (h + 1) * 128
                    ]
            return carry

        lax.fori_loop(0, bond_dim, one_left, 0, unroll=4)
        for h in range(halves):
            out_ref[:, :, h * 128 : (h + 1) * 128] = (
                scratch[h].astype(jnp.bfloat16).reshape(bond_dim, out_rows, 128)
            )

    return pl.pallas_call(
        body,
        grid=(tiles,),
        in_specs=[
            pl.BlockSpec((rows, TILE), lambda t: (0, t)),
            pl.BlockSpec(left_tiled.shape, lambda t: (0, 0, 0)),
        ],
        out_specs=pl.BlockSpec((bond_dim, out_rows, TILE), lambda t: (0, 0, t)),
        out_shape=jax.ShapeDtypeStruct((bond_dim, out_rows, padded), jnp.bfloat16),
        scratch_shapes=[pltpu.VMEM((halves, bond_dim * out_rows, 128), jnp.float32)],
        compiler_params=pltpu.CompilerParams(vmem_limit_bytes=VMEM_LIMIT),
        name="weight_upper",
    )(upper_part, left_tiled)


def contract(weighted, lower, right_tiled, bond_dim, group, step):
    out_rows, padded = weighted.shape[1:]
    in_rows, in_cols = lower.shape
    span = group * bond_dim
    row_tiles = padded // TILE
    col_tiles = -(-in_cols // span)
    steps = bond_dim // step

    def body(w_ref, lower_ref, right_ref, out_ref, lower_pad, acc):
        @pl.when(pl.program_id(0) == 0)
        def _():
            lower_pad[...] = jnp.zeros_like(lower_pad)
            acc[...] = jnp.zeros_like(acc)
            for i in range(row_tiles):
                height = min(span, in_rows - i * span)
                for j in range(col_tiles):
                    width = min(span, in_cols - j * span)
                    lower_pad[i * TILE : i * TILE + height, j * TILE : j * TILE + width] = lower_ref[
                        i * span : i * span + height, j * span : j * span + width
                    ]

        weights = jnp.concatenate(
            [block_diagonal(right_ref[k], group) for k in range(step)], axis=0
        )
        left = w_ref[...].reshape(step * out_rows, padded)
        for j in range(col_tiles):
            cols = slice(j * TILE, (j + 1) * TILE)
            paired = jnp.dot(left, lower_pad[:, cols], preferred_element_type=jnp.float32)
            paired = paired.astype(jnp.bfloat16)
            wide = jnp.concatenate(
                [paired[k * out_rows : (k + 1) * out_rows] for k in range(step)], axis=1
            )
            acc[:, cols] += jnp.dot(wide, weights, preferred_element_type=jnp.float32)

        @pl.when(pl.program_id(0) == steps - 1)
        def _():
            for j in range(col_tiles):
                width = min(span, in_cols - j * span)
                out_ref[:, j * span : j * span + width] = acc[
                    :, j * TILE : j * TILE + width
                ].astype(jnp.bfloat16)

    return pl.pallas_call(
        body,
        grid=(steps,),
        in_specs=[
            pl.BlockSpec((step, out_rows, padded), lambda r: (r, 0, 0)),
            pl.BlockSpec((in_rows, in_cols), lambda r: (0, 0)),
            pl.BlockSpec((step, bond_dim, TILE), lambda r: (r, 0, 0)),
        ],
        out_specs=pl.BlockSpec((out_rows, in_cols), lambda r: (0, 0)),
        out_shape=jax.ShapeDtypeStruct((out_rows, in_cols), jnp.bfloat16),
        scratch_shapes=[
            pltpu.VMEM((padded, col_tiles * TILE), jnp.bfloat16),
            pltpu.VMEM((out_rows, col_tiles * TILE), jnp.float32),
        ],
        compiler_params=pltpu.CompilerParams(vmem_limit_bytes=VMEM_LIMIT),
        name="contract",
    )(weighted, lower, right_tiled)


def local(top_tensor, bottom_tensor, left_proj, right_proj):
    bond_dim = right_proj.shape[1]
    rows_here = top_tensor.shape[0]
    if rows_here % bond_dim or bond_dim % 16 or bond_dim > TILE:
        return local_windowed(top_tensor, bottom_tensor, left_proj, right_proj)
    block_len = top_tensor.shape[1] // bond_dim
    ups = rows_here // bond_dim
    group = TILE // bond_dim
    chunk_cols = bottom_tensor.shape[1] // CHUNKS
    lowers = [
        lax.all_gather(
            bottom_tensor[:, c * chunk_cols : (c + 1) * chunk_cols], "row", axis=0, tiled=True
        )
        for c in range(CHUNKS)
    ]
    left_tiled = tiled_blocks(
        left_proj.reshape(bond_dim, bond_dim, bond_dim).transpose(2, 0, 1), group
    )
    right_tiled = tiled_blocks(right_proj.reshape(bond_dim, bond_dim, bond_dim), group)
    tiles = -(-block_len // group)
    span = group * bond_dim
    upper_part = jnp.pad(top_tensor, ((0, 0), (0, tiles * span - top_tensor.shape[1])))
    upper_part = jnp.pad(
        upper_part.reshape(rows_here, tiles, span), ((0, 0), (0, 0), (0, TILE - span))
    ).reshape(rows_here, tiles * TILE)
    weighted = weight_upper(upper_part, left_tiled, bond_dim, ups, group)
    step = 4
    parts = [contract(weighted, lower, right_tiled, bond_dim, group, step) for lower in lowers]
    partial = jnp.concatenate(parts, axis=1).reshape(ups, bond_dim, bond_dim, bond_dim)
    partial = partial.transpose(2, 1, 0, 3).reshape(bond_dim * bond_dim, ups * bond_dim)
    arrived = lax.all_to_all(partial, ("col", "row"), split_axis=0, concat_axis=0, tiled=True)
    cols, row_count = lax.axis_size("col"), lax.axis_size("row")
    out_rows = bond_dim * bond_dim // (cols * row_count)
    arrived = arrived.reshape(cols, row_count, out_rows, ups * bond_dim)
    combined = jnp.sum(arrived.astype(jnp.float32), axis=0).astype(jnp.bfloat16)
    return combined.transpose(1, 0, 2).reshape(out_rows, bond_dim * bond_dim)


def solution(mesh):
    return jax.shard_map(
        local,
        mesh=mesh,
        in_specs=(P("row", "col"), P(("col", "row"), None), P(), P()),
        out_specs=P(("col", "row"), None),
        check_vma=False,
    )
```
